256 devices in a mesh: dp: 16 (over z, core), mp: 16 (over y, x).
Axes of the slice: x: 4, y: 4, z: 8, core: 2. Of those that a mesh axis runs over, the one named last changes fastest.
Arguments:
- records: bfloat16 [1024, 128, 1024], P(('dp', 'mp')), may hold values from -21 to 21
- w_query: bfloat16 [1024, 1024], replicated, may hold values from -0.1875 to 0.1875
- w_key: bfloat16 [1024, 1024], replicated, may hold values from -0.1875 to 0.1875
- w_value: bfloat16 [1024, 1024], replicated, may hold values from -0.1875 to 0.1875
- pair_owner: int32 [1024], P(('dp', 'mp')), may hold values from 0 to 1023, as said below
- pair_partner: int32 [1024], P(('dp', 'mp')), may hold values from 0 to 1023, as said below
- confidence: int32 [1024], P(('dp', 'mp')), may hold values from 16 to 256
- labels: int32 [1024], P(('dp', 'mp')), may hold values from 0 to 1
Outputs:
- loss: float32 [], replicated
- record_grad: float32 [1024, 128, 1024], P(('dp', 'mp'))
The draws below stay inside these ranges and needn't reach their ends.
Inputs may be any that keep to these rules, and one draw needn't show every extreme that they name: `pair_owner`: the 4 pairs held by a device have their owners among the records held by that device. `pair_partner`: a partner follows its owner by 1 to 8 records in the circular record order (ids taken modulo 1024); in every draw some pair's partner is exactly 8 records after its owner.
All inputs are finite; a program needn't handle non-finite values.
Results may differ from the reference program's by a relative error of at most 0.03.
The reference program's roundings to bfloat16 on the way count: a program that leaves them out, or rounds other values in their place, can miss the bound.
Values may be sent and summed in bfloat16 or wider, within the bound.
No kernel may reach another device: no remote copies, remote signals or barrier semaphores. Data moves between devices by JAX's collectives and lax.ppermute only.
A program may use at most 128 MiB of HBM per device.

```python
import jax
import jax.numpy as jnp
from jax import lax

D = 1024
HEADS = 16
SEQ = 128
R_DEV = 4
NREC = 1024
NPAIRS = 1024
WIN = 8


def draw_records(key, part):
    first_key = jax.random.fold_in(key, 0)
    base = jnp.clip(jax.random.normal(first_key, (NREC, SEQ, D), jnp.float32), -6.0, 6.0)
    return base.astype(jnp.bfloat16)


def pair_ids(key):
    base_key = jax.random.fold_in(key, 7)
    owner_key, offset_key, pick_key = jax.random.split(base_key, 3)
    index = jnp.arange(NPAIRS, dtype=jnp.int32)
    owners = index // R_DEV * R_DEV + jax.random.randint(owner_key, (NPAIRS,), 0, R_DEV, jnp.int32)
    offsets = jax.random.randint(offset_key, (NPAIRS,), 1, WIN + 1, jnp.int32)
    picked = jax.random.randint(pick_key, (), 0, NPAIRS, jnp.int32)
    offsets = jnp.where(index == picked, WIN, offsets)
    partners = jnp.mod(owners + offsets, NREC)
    return (owners.astype(jnp.int32), partners.astype(jnp.int32))


def draw_pair_owner(key, part):
    return pair_ids(key)[0]


def draw_pair_partner(key, part):
    return pair_ids(key)[1]


def draw_confidence(key, part):
    conf_key = jax.random.fold_in(key, 11)
    index = jnp.arange(NPAIRS, dtype=jnp.int32)
    upper = 32 + 224 * index // max(NPAIRS - 1, 1)
    lower = upper // 2
    raw = jax.random.randint(conf_key, (NPAIRS,), 0, 1 << 20, jnp.int32)
    values = lower + jnp.mod(raw, upper - lower + 1)
    values = jnp.where(index == 0, 16, values)
    values = jnp.where(index == NPAIRS - 1, 256, values)
    return values.astype(jnp.int32)


def touch_ends(array, own_key, least, largest):
    dims = array.shape
    index_at = [jax.random.randint(jax.random.fold_in(own_key, axis), (), 0, dims[axis]) for axis in range(len(dims))]
    array = array.at[tuple(index_at)].set(least)
    longest = dims.index(max(dims))
    index_at[longest] = (index_at[longest] + 1) % dims[longest]
    return array.at[tuple(index_at)].set(largest)


def scatter_about(own_key, shape, deviation, limit, kind=jnp.bfloat16):
    drawn = jax.random.normal(own_key, shape, jnp.float32) * deviation
    return jnp.minimum(jnp.maximum(drawn, -limit), limit).astype(kind)


def setup_inputs(seed: int = 0) -> dict:
    splits = jax.random.split(jax.random.key(seed), 9)
    records = draw_records(jax.random.fold_in(splits[8], 71), 0)
    w_query = scatter_about(splits[1], (D, D), D ** -0.5, 0.1875)
    w_key = scatter_about(splits[2], (D, D), D ** -0.5, 0.1875)
    w_value = scatter_about(splits[3], (D, D), D ** -0.5, 0.1875)
    pair_owner = draw_pair_owner(jax.random.fold_in(splits[8], 71), 0)
    pair_partner = draw_pair_partner(jax.random.fold_in(splits[8], 71), 0)
    confidence = draw_confidence(jax.random.fold_in(splits[8], 71), 0)
    labels = touch_ends(jax.random.randint(splits[7], (NPAIRS,), 0, 2), jax.random.fold_in(splits[7], 1), 0, 1).astype(jnp.int32)
    return {"records": records, "w_query": w_query, "w_key": w_key, "w_value": w_value, "pair_owner": pair_owner, "pair_partner": pair_partner, "confidence": confidence, "labels": labels}


def attend(query, keys, values):
    size = keys.shape[-1] // HEADS
    qh = query.astype(jnp.float32).reshape(query.shape[0], HEADS, size)
    kh = keys.astype(jnp.float32).reshape(keys.shape[0], HEADS, size)
    vh = values.astype(jnp.float32).reshape(values.shape[0], HEADS, size)
    scores = jnp.einsum('qhd,khd->hqk', qh, kh) / jnp.sqrt(jnp.float32(size))
    chance = jax.nn.softmax(scores, axis=-1).astype(jnp.bfloat16)
    mixed = jnp.einsum('hqk,khd->qhd', chance.astype(jnp.float32), vh)
    return lax.optimization_barrier(jnp.mean(mixed, axis=0))

def pair_link(q_own, k_own, v_own, q_other, k_other, v_other):
    return 4.0 * jnp.sum(attend(q_own, k_other, v_other) * attend(q_other, k_own, v_own))

def reference(records, w_query, w_key, w_value, pair_owner, pair_partner, confidence, labels):
    flat_rows = records.reshape(NREC * SEQ, D).astype(jnp.float32)

    def project(weight):
        out = jnp.dot(flat_rows, weight.astype(jnp.float32), precision=lax.Precision.HIGHEST)
        return out.astype(jnp.bfloat16).reshape(NREC, SEQ, D)
    all_q = project(w_query)
    all_k = project(w_key)
    all_v = project(w_value)

    def one_block(items):
        owners, partners, conf, label = items
        inputs = (all_q[owners], all_k[owners], all_v[owners], all_q[partners], all_k[partners], all_v[partners])
        link_z, pullback = jax.vjp(jax.vmap(pair_link), *inputs)
        weight = conf.astype(jnp.float32) / 256.0
        target = label.astype(jnp.float32)
        part_loss = jnp.sum(weight * (jax.nn.softplus(link_z) - target * link_z))
        pair_cotangent = SEQ * weight * (jax.nn.sigmoid(link_z) - target)
        grads = pullback(pair_cotangent.astype(link_z.dtype))
        return (part_loss,) + tuple(grads)
    blocks = NPAIRS // R_DEV
    items = (pair_owner.reshape(blocks, R_DEV), pair_partner.reshape(blocks, R_DEV), confidence.reshape(blocks, R_DEV), labels.reshape(blocks, R_DEV))
    outs = lax.map(one_block, items)
    loss = jnp.sum(outs[0]) / NPAIRS
    grads = [g.reshape(NPAIRS * SEQ, D) for g in outs[1:]]
    weights = [w_query, w_key, w_value]

    def back(three):
        total = jnp.zeros((NPAIRS * SEQ, D), jnp.float32)
        for grad_part, weight in zip(three, weights):
            total = total + jnp.dot(grad_part.astype(jnp.float32), weight.astype(jnp.float32).T, precision=lax.Precision.HIGHEST)
        return total.reshape(NPAIRS, SEQ, D)
    record_grad = jnp.zeros((NREC, SEQ, D), jnp.float32)
    record_grad = record_grad.at[pair_owner].add(back(grads[0:3]))
    partner_terms = back(grads[3:6])
    pair_block = jnp.arange(NPAIRS, dtype=jnp.int32) // R_DEV
    distance = jnp.mod(pair_partner // R_DEV - pair_block, NREC // R_DEV)
    for step in range(3):
        chosen = (distance == step).astype(jnp.float32)[:, None, None]
        group = jnp.zeros((NREC, SEQ, D), jnp.float32).at[pair_partner].add(partner_terms * chosen)
        if step > 0:
            group = group.astype(jnp.bfloat16).astype(jnp.float32)
        record_grad = record_grad + group
    return (loss, record_grad)
```

```python
import functools

import jax
import jax.numpy as jnp
from jax import lax
from jax.experimental import pallas as pl
from jax.experimental.pallas import tpu as pltpu
from jax.sharding import PartitionSpec as P

AXES = ("dp", "mp")
HEADS = 16
LOG2_E = 1.4426950408889634
NT = (((1,), (1,)), ((), ()))
TN = (((0,), (0,)), ((), ()))
VMEM = pl.BlockSpec(memory_space=pltpu.VMEM)
SMEM = pl.BlockSpec(memory_space=pltpu.SMEM)
ANY = pl.BlockSpec(memory_space=pl.ANY)


def mm(a, b, dims=(((1,), (0,)), ((), ()))):
    return lax.dot_general(a, b, dims, preferred_element_type=jnp.float32)


def from_behind(block, distance):
    count = lax.axis_size(AXES)
    return lax.ppermute(block, AXES, [((i - distance) % count, i) for i in range(count)])


def project_kernel(x_ref, wq_ref, wk_ref, wv_ref, out_ref, *, tile):
    width = x_ref.shape[1]
    for n, w_ref in enumerate((wq_ref, wk_ref, wv_ref)):

        def columns(i, _, n=n, w_ref=w_ref):
            at = pl.multiple_of(i * tile, tile)
            made = mm(x_ref[...], w_ref[:, pl.ds(at, tile)])
            out_ref[:, pl.ds(pl.multiple_of(n * width + at, tile), tile)] = made.astype(jnp.bfloat16)
            return 0

        lax.fori_loop(0, width // tile, columns, 0)


def project(records, weights):
    count, seq, width = records.shape
    out = pl.pallas_call(
        functools.partial(project_kernel, tile=256),
        out_shape=jax.ShapeDtypeStruct((count * seq, 3 * width), jnp.bfloat16),
        in_specs=[VMEM] * 4,
        out_specs=VMEM,
        compiler_params=pltpu.CompilerParams(vmem_limit_bytes=40 << 20),
        cost_estimate=pl.CostEstimate(
            flops=6 * count * seq * width * width, bytes_accessed=14 << 20, transcendentals=0
        ),
        name="project",
    )(records.reshape(count * seq, width), *weights)
    return out.reshape(count, seq, 3 * width)


def attend(q, k, v, first, ends):
    zero = jnp.zeros_like(q)
    qs = jnp.concatenate([jnp.where(first, q, zero), jnp.where(first, zero, q)], axis=0)
    scores = mm(k, qs, NT)
    top = jnp.max(scores, axis=0, keepdims=True)
    e = jnp.exp2((scores - top) * (LOG2_E / 8.0))
    p = e * (1.0 / jnp.sum(e, axis=0, keepdims=True))
    mass = mm(p.astype(jnp.bfloat16), ends)
    pooled = jnp.sum(mass * v.astype(jnp.float32), axis=0, keepdims=True) * (1.0 / k.shape[0])
    return qs, p, mass, pooled


def attend_back(dp, qs, p, mass, k, v, first):
    dv = (mass * dp).astype(jnp.bfloat16)
    dpb = jnp.broadcast_to((dp * 0.125).astype(jnp.bfloat16), k.shape)
    zero = jnp.zeros_like(dpb)
    spread = jnp.concatenate([jnp.where(first, dpb, zero), jnp.where(first, zero, dpb)], axis=0)
    t = mm(v, spread, NT).astype(jnp.bfloat16).astype(jnp.float32)
    r = jnp.sum(p * t, axis=0, keepdims=True)
    ds = (p * (t - r)).astype(jnp.bfloat16)
    dk = mm(ds, qs).astype(jnp.bfloat16)
    both = mm(ds, k, TN)
    seq = k.shape[0]
    dq = jnp.where(first, both[:seq], both[seq:]).astype(jnp.bfloat16)
    return dq, dk, dv


def pairs_kernel(info_ref, left_ref, own_ref, right_ref, grads_ref, z_ref, a_buf, b_buf, sems):
    count, seq, full = a_buf.shape
    recs = left_ref.shape[0]
    width = full // 3

    def copy_a(p):
        return pltpu.make_async_copy(left_ref.at[info_ref[p]], a_buf.at[p], sems.at[0, p])

    def copy_b(p, source, slot):
        return pltpu.make_async_copy(source.at[slot], b_buf.at[p], sems.at[1, p])

    for p in range(count):
        copy_a(p).start()
        slot = info_ref[count + p]
        for n, source in enumerate((left_ref, own_ref, right_ref)):

            @pl.when((slot >= n * recs) & (slot < (n + 1) * recs))
            def _(p=p, n=n, source=source, slot=slot):
                copy_b(p, source, slot - n * recs).start()

    lane = lax.broadcasted_iota(jnp.int32, (seq, 128), 1)
    first = lane < 64
    row = lax.broadcasted_iota(jnp.int32, (2 * seq, 128), 0)
    col = lax.broadcasted_iota(jnp.int32, (2 * seq, 128), 1)
    ends = jnp.where((row < seq) == (col < 64), 1.0, 0.0).astype(jnp.bfloat16)
    for p in range(count):
        copy_a(p).wait()
        copy_b(p, own_ref, 0).wait()
        a, b = a_buf.at[p], b_buf.at[p]

        def head_pair(i, z, a=a, b=b, p=p):
            at = [pl.ds(pl.multiple_of(n * width + i * 128, 128), 128) for n in range(3)]
            qa, ka, va = (a[:, s] for s in at)
            qb, kb, vb = (b[:, s] for s in at)
            qs_ab, p_ab, mass_ab, pooled_ab = attend(qa, kb, vb, first, ends)
            qs_ba, p_ba, mass_ba, pooled_ba = attend(qb, ka, va, first, ends)
            z = z + pooled_ab * pooled_ba
            unit = 4.0 / seq
            dqa, dkb, dvb = attend_back(pooled_ba * unit, qs_ab, p_ab, mass_ab, kb, vb, first)
            dqb, dka, dva = attend_back(pooled_ab * unit, qs_ba, p_ba, mass_ba, ka, va, first)
            for s, value in zip(at, (dqa, dka, dva)):
                grads_ref[pl.ds(p * seq, seq), s] = value
            for s, value in zip(at, (dqb, dkb, dvb)):
                grads_ref[pl.ds((count + p) * seq, seq), s] = value
            return z

        z = lax.fori_loop(0, width // 128, head_pair, jnp.zeros((1, 128), jnp.float32))
        z_ref[p] = 4.0 * jnp.sum(z)


def pairs(info, left, own, right, count):
    recs, seq, full = own.shape
    return pl.pallas_call(
        pairs_kernel,
        out_shape=(
            jax.ShapeDtypeStruct((2 * count * seq, full), jnp.bfloat16),
            jax.ShapeDtypeStruct((count,), jnp.float32),
        ),
        in_specs=[SMEM, ANY, ANY, ANY],
        out_specs=(VMEM, SMEM),
        scratch_shapes=[
            pltpu.VMEM((count, seq, full), jnp.bfloat16),
            pltpu.VMEM((count, seq, full), jnp.bfloat16),
            pltpu.SemaphoreType.DMA((2, count)),
        ],
        compiler_params=pltpu.CompilerParams(vmem_limit_bytes=40 << 20),
        cost_estimate=pl.CostEstimate(flops=12 << 30, bytes_accessed=12 << 20, transcendentals=2 << 20),
        name="pairs",
    )(info, left, own, right)


def terms_kernel(info_ref, z_ref, g_ref, wq_ref, wk_ref, wv_ref, left_ref, own_ref, right_ref, acc, *, tile, count, recs):
    seq = g_ref.shape[0] // (2 * count)
    width = wq_ref.shape[1]
    scales = []
    for p in range(count):
        z = jnp.full((8, 128), z_ref[p], jnp.float32)
        c = info_ref[2 * count + p].astype(jnp.float32) * (1.0 / 256.0)
        y = info_ref[3 * count + p].astype(jnp.float32)
        scales.append((seq * c * (jax.nn.sigmoid(z) - y))[0:1, 0:1])

    def columns(i, _):
        at = pl.multiple_of(i * tile, tile)
        made = None
        for n, w_ref in enumerate((wq_ref, wk_ref, wv_ref)):
            part = mm(g_ref[:, n * width : (n + 1) * width], w_ref[pl.ds(at, tile), :], NT)
            made = part if made is None else made + part
        acc[...] = jnp.zeros_like(acc)
        for n in range(2 * count):
            slot = info_ref[n]
            acc[slot] += made[n * seq : (n + 1) * seq] * scales[n % count]
        for n, out in enumerate((left_ref, own_ref, right_ref)):
            out[:, :, pl.ds(at, tile)] = acc[n * recs : (n + 1) * recs].astype(jnp.bfloat16)
        return 0

    lax.fori_loop(0, wq_ref.shape[0] // tile, columns, 0)


def terms(info, z, grads, weights, recs, count):
    seq = grads.shape[0] // (2 * count)
    width, columns = weights[0].shape[1], weights[0].shape[0]
    made = jax.ShapeDtypeStruct((recs, seq, columns), jnp.bfloat16)
    tile = 256
    return pl.pallas_call(
        functools.partial(terms_kernel, tile=tile, count=count, recs=recs),
        out_shape=(made, made, made),
        in_specs=[SMEM, SMEM] + [VMEM] * 4,
        out_specs=(VMEM,) * 3,
        scratch_shapes=[pltpu.VMEM((3 * recs, seq, tile), jnp.float32)],
        compiler_params=pltpu.CompilerParams(vmem_limit_bytes=40 << 20),
        cost_estimate=pl.CostEstimate(
            flops=2 * grads.shape[0] * 3 * width * columns, bytes_accessed=20 << 20, transcendentals=0
        ),
        name="terms",
    )(info, z, grads, *weights)


def total_over_devices(value):
    count, step = lax.axis_size(AXES), 1
    while step < count:
        value = value + lax.ppermute(value, AXES, [(i, i ^ step) for i in range(count)])
        step *= 2
    return value


def on_device(records, w_query, w_key, w_value, pair_owner, pair_partner, confidence, labels):
    recs, seq, width = records.shape
    count = pair_owner.shape[0]
    devices = lax.axis_size(AXES)
    first_id = lax.axis_index(AXES) * recs
    weights = (w_query, w_key, w_value)

    own_info = jnp.concatenate(
        [pair_owner - first_id, jnp.mod(pair_partner - first_id, recs * devices), confidence, labels]
    )
    info = from_behind(own_info, 1)
    left_records = from_behind(records, 1)
    right_records = from_behind(records, -1)
    own = project(records, weights)
    left = project(left_records, weights)
    right = project(right_records, weights)

    grads, z = pairs(info, left, own, right, count)
    to_left, kept, to_right = terms(info, z, grads, weights, recs, count)
    from_right = from_behind(to_left, -1)
    from_left = from_behind(to_right, 1)

    c = info[2 * count : 3 * count].astype(jnp.float32) / 256.0
    y = info[3 * count :].astype(jnp.float32)
    loss = jnp.sum(c * (jax.nn.softplus(z) - y * z))
    loss = total_over_devices(loss) / (count * devices)
    record_grad = (
        from_right.astype(jnp.float32) + kept.astype(jnp.float32) + from_left.astype(jnp.float32)
    )
    return (loss, record_grad)


def solution(mesh):
    blocks = P(AXES, None, None)
    in_specs = (blocks, P(), P(), P(), P(AXES), P(AXES), P(AXES), P(AXES))
    return jax.shard_map(
        on_device, mesh=mesh, in_specs=in_specs, out_specs=(P(), blocks), check_vma=False
    )
```

```python
import functools

import jax
import jax.numpy as jnp
from jax import lax
from jax.experimental import pallas as pl
from jax.experimental.pallas import tpu as pltpu
from jax.sharding import PartitionSpec as P

AXES = ("dp", "mp")
LATE = 1
LOG2_E = 1.4426950408889634
NT = (((1,), (1,)), ((), ()))
TN = (((0,), (0,)), ((), ()))
VMEM = pl.BlockSpec(memory_space=pltpu.VMEM)
SMEM = pl.BlockSpec(memory_space=pltpu.SMEM)
ANY = pl.BlockSpec(memory_space=pl.ANY)


def mm(a, b, dims=(((1,), (0,)), ((), ()))):
    return lax.dot_general(a, b, dims, preferred_element_type=jnp.float32)


def from_behind(block, distance):
    count = lax.axis_size(AXES)
    return lax.ppermute(block, AXES, [((i - distance) % count, i) for i in range(count)])


def project_kernel(*refs):
    blocks = (len(refs) - 3) // 2
    xs, weights, outs = refs[:blocks], refs[blocks : blocks + 3], refs[blocks + 3 :]
    for n, w_ref in enumerate(weights):
        for x_ref, out_ref in zip(xs, outs):
            recs, seq, width = x_ref.shape
            made = mm(x_ref[...].reshape(recs * seq, width), w_ref[...])
            out_ref[:, :, n * width : (n + 1) * width] = made.astype(jnp.bfloat16).reshape(recs, seq, width)


def project(blocks, weights):
    rows = sum(block.shape[0] * block.shape[1] for block in blocks)
    width = blocks[0].shape[2]
    return pl.pallas_call(
        project_kernel,
        out_shape=[jax.ShapeDtypeStruct(block.shape[:2] + (3 * width,), jnp.bfloat16) for block in blocks],
        in_specs=[VMEM] * (len(blocks) + 3),
        out_specs=[VMEM] * len(blocks),
        compiler_params=pltpu.CompilerParams(vmem_limit_bytes=18 << 20),
        cost_estimate=pl.CostEstimate(flops=6 * rows * width * width, bytes_accessed=14 << 20, transcendentals=0),
        name="project",
    )(*blocks, *weights)


def pairs_kernel(
    info_ref, left_ref, own_ref, right_ref, left_x, right_x, wq_ref, wk_ref, wv_ref, grads_ref, z_ref, win, sems, *, count
):
    total, seq, full = win.shape
    recs, early, late = own_ref.shape[0], left_ref.shape[0], left_x.shape[0]
    width = full // 3
    copies = [
        pltpu.make_async_copy(ref, win.at[pl.ds(start, ref.shape[0])], sems.at[n])
        for n, (ref, start) in enumerate(((left_ref, 0), (own_ref, recs), (right_ref, 2 * recs)))
    ]
    for copy in copies:
        copy.start()
    rows = late * seq
    x = jnp.concatenate([left_x[...].reshape(rows, width), right_x[...].reshape(rows, width)], axis=0)
    for n, w_ref in enumerate((wq_ref, wk_ref, wv_ref)):
        made = mm(x, w_ref[...]).astype(jnp.bfloat16)
        at = slice(n * width, (n + 1) * width)
        win[early:recs, :, at] = made[:rows].reshape(late, seq, width)
        win[2 * recs + early :, :, at] = made[rows:].reshape(late, seq, width)

    lane = lax.broadcasted_iota(jnp.int32, (seq, 128), 1)
    first = lane < 64
    row = lax.broadcasted_iota(jnp.int32, (2 * seq, 128), 0)
    col = lax.broadcasted_iota(jnp.int32, (2 * seq, 128), 1)
    ends = jnp.where((row < seq) == (col < 64), 1.0, 0.0).astype(jnp.bfloat16)
    zero = jnp.zeros((seq, 128), jnp.bfloat16)
    for copy in copies:
        copy.wait()

    def one_pair(p, _):
        a, b = info_ref[p], info_ref[count + p]
        jobs = []
        for i in range(width // 128):
            at = [slice(n * width + i * 128, n * width + (i + 1) * 128) for n in range(3)]
            qa, ka, va = (win[a, :, s] for s in at)
            qb, kb, vb = (win[b, :, s] for s in at)
            jobs.append((at, 0, count, qa, kb, vb))
            jobs.append((at, count, 0, qb, ka, va))
        qs = [
            jnp.concatenate([jnp.where(first, job[3], zero), jnp.where(first, zero, job[3])], axis=0) for job in jobs
        ]
        scores = [mm(job[4], q, NT) for job, q in zip(jobs, qs)]
        probs = []
        for s in scores:
            top = jnp.max(s, axis=0, keepdims=True)
            e = jnp.exp2((s - top) * (LOG2_E / 8.0))
            probs.append(e * (1.0 / jnp.sum(e, axis=0, keepdims=True)))
        mass = [mm(prob.astype(jnp.bfloat16), ends) for prob in probs]
        pooled = [
            jnp.sum(m * job[5].astype(jnp.float32), axis=0, keepdims=True) * (1.0 / seq) for m, job in zip(mass, jobs)
        ]
        z = jnp.zeros((1, 128), jnp.float32)
        for i in range(width // 128):
            z = z + pooled[2 * i] * pooled[2 * i + 1]
        z_ref[p] = 4.0 * jnp.sum(z)
        dps = [pooled[n ^ 1] * (4.0 / seq) for n in range(len(jobs))]
        ts = [
            mm((job[5].astype(jnp.float32) * (dp * 0.125)).astype(jnp.bfloat16), ends, NT)
            for dp, job in zip(dps, jobs)
        ]
        dss = []
        for prob, t in zip(probs, ts):
            r = jnp.sum(prob * t, axis=0, keepdims=True)
            dss.append((prob * (t - r)).astype(jnp.bfloat16))
        dks = [mm(ds, q) for ds, q in zip(dss, qs)]
        dqs = [mm(ds, job[4], TN) for ds, job in zip(dss, jobs)]
        for n, (at, qrow, krow, _, _, _) in enumerate(jobs):
            grads_ref[krow + p, :, at[2]] = (mass[n] * dps[n]).astype(jnp.bfloat16)
            grads_ref[krow + p, :, at[1]] = dks[n].astype(jnp.bfloat16)
            grads_ref[qrow + p, :, at[0]] = jnp.where(first, dqs[n][:seq], dqs[n][seq:]).astype(jnp.bfloat16)
        return 0

    lax.fori_loop(0, count, one_pair, 0)


def pairs(info, left, own, right, left_x, right_x, weights, count):
    recs, seq, full = own.shape
    return pl.pallas_call(
        functools.partial(pairs_kernel, count=count),
        out_shape=(
            jax.ShapeDtypeStruct((2 * count, seq, full), jnp.bfloat16),
            jax.ShapeDtypeStruct((count,), jnp.float32),
        ),
        in_specs=[SMEM, ANY, ANY, ANY] + [VMEM] * 5,
        out_specs=(VMEM, SMEM),
        scratch_shapes=[pltpu.VMEM((3 * recs, seq, full), jnp.bfloat16), pltpu.SemaphoreType.DMA((3,))],
        compiler_params=pltpu.CompilerParams(vmem_limit_bytes=28 << 20),
        cost_estimate=pl.CostEstimate(flops=12 << 30, bytes_accessed=12 << 20, transcendentals=2 << 20),
        name="pairs",
    )(info, left, own, right, left_x, right_x, *weights)


def terms_kernel(
    info_ref, z_ref, g_ref, wq_ref, wk_ref, wv_ref, left_ref, own_ref, right_ref, acc, *, columns, count, recs
):
    _, seq, full = g_ref.shape
    width = full // 3
    made = None
    for n, w_ref in enumerate((wq_ref, wk_ref, wv_ref)):
        grads = g_ref[:, :, n * width : (n + 1) * width].reshape(2 * count * seq, width)
        part = mm(grads, w_ref[columns, :], NT)
        made = part if made is None else made + part
    acc[...] = jnp.zeros_like(acc)
    for n in range(2 * count):
        p = n % count
        z = jnp.full((8, 128), z_ref[p], jnp.float32)
        c = info_ref[2 * count + p].astype(jnp.float32) * (1.0 / 256.0)
        y = info_ref[3 * count + p].astype(jnp.float32)
        g = (seq * c * (jax.nn.sigmoid(z) - y))[0:1, 0:1]
        acc[info_ref[n]] += made[n * seq : (n + 1) * seq] * g
    for n, out in enumerate((left_ref, own_ref, right_ref)):
        out[...] = acc[n * recs : (n + 1) * recs].astype(jnp.bfloat16)


def terms(info, z, grads, weights, recs, count, columns):
    _, seq, full = grads.shape
    size = columns.stop - columns.start
    made = jax.ShapeDtypeStruct((recs, seq, size), jnp.bfloat16)
    return pl.pallas_call(
        functools.partial(terms_kernel, columns=columns, count=count, recs=recs),
        out_shape=(made, made, made),
        in_specs=[SMEM, SMEM] + [VMEM] * 4,
        out_specs=(VMEM,) * 3,
        scratch_shapes=[pltpu.VMEM((3 * recs, seq, size), jnp.float32)],
        compiler_params=pltpu.CompilerParams(vmem_limit_bytes=18 << 20),
        cost_estimate=pl.CostEstimate(
            flops=4 * count * seq * full * size, bytes_accessed=12 << 20, transcendentals=0
        ),
        name="terms",
    )(info, z, grads, *weights)


def swap(value, step):
    return value + lax.ppermute(value, AXES, [(i, i ^ step) for i in range(lax.axis_size(AXES))])


def on_device(records, w_query, w_key, w_value, pair_owner, pair_partner, confidence, labels):
    recs, seq, width = records.shape
    count = pair_owner.shape[0]
    devices = lax.axis_size(AXES)
    first_id = lax.axis_index(AXES) * recs
    weights = (w_query, w_key, w_value)
    early = recs - LATE

    left_early, right_early = (from_behind(records[:early], d) for d in (1, -1))
    left_late, right_late = (from_behind(records[early:], d) for d in (1, -1))
    own_info = jnp.concatenate(
        [pair_owner - first_id, jnp.mod(pair_partner - first_id, recs * devices), confidence, labels]
    )
    info = from_behind(own_info, 1)
    (own,) = project([records], weights)
    left, right = project([left_early, right_early], weights)
    grads, z = pairs(info, left, own, right, left_late, right_late, weights, count)

    c = info[2 * count : 3 * count].astype(jnp.float32) / 256.0
    y = info[3 * count :].astype(jnp.float32)
    loss = jnp.sum(c * (jax.nn.softplus(z) - y * z))
    z, loss = lax.optimization_barrier((z, loss))
    half = width // 2
    loss = swap(loss, 1)
    to_left, kept_a, to_right = terms(info, z, grads, weights, recs, count, slice(0, half))
    to_left, to_right, z, loss = lax.optimization_barrier((to_left, to_right, z, loss))
    loss = swap(loss, 2)
    from_right_a, from_left_a = from_behind(to_left, -1), from_behind(to_right, 1)
    to_left, kept_b, to_right = terms(info, z, grads, weights, recs, count, slice(half, width))
    to_left, to_right, loss = lax.optimization_barrier((to_left, to_right, loss))
    from_right_b, from_left_b = from_behind(to_left, -1), from_behind(to_right, 1)
    step = devices // 2
    while step > 2:
        loss = swap(loss, step)
        step //= 2
    loss = loss / (count * devices)

    def added(first, second, third):
        return first.astype(jnp.float32) + second.astype(jnp.float32) + third.astype(jnp.float32)

    record_grad = jnp.concatenate(
        [added(from_right_a, kept_a, from_left_a), added(from_right_b, kept_b, from_left_b)], axis=2
    )
    return (loss, record_grad)


def solution(mesh):
    blocks = P(AXES, None, None)
    in_specs = (blocks, P(), P(), P(), P(AXES), P(AXES), P(AXES), P(AXES))
    return jax.shard_map(
        on_device, mesh=mesh, in_specs=in_specs, out_specs=(P(), blocks), check_vma=False
    )
```

```python
import functools

import jax
import jax.numpy as jnp
from jax import lax
from jax.experimental import pallas as pl
from jax.experimental.pallas import tpu as pltpu
from jax.sharding import PartitionSpec as P

AXES = ("dp", "mp")
ROW = 4
LOG2_E = 1.4426950408889634
NT = (((1,), (1,)), ((), ()))
TN = (((0,), (0,)), ((), ()))
VMEM = pl.BlockSpec(memory_space=pltpu.VMEM)
SMEM = pl.BlockSpec(memory_space=pltpu.SMEM)
ANY = pl.BlockSpec(memory_space=pl.ANY)


def mm(a, b, dims=(((1,), (0,)), ((), ()))):
    return lax.dot_general(a, b, dims, preferred_element_type=jnp.float32)


def from_behind(block, distance):
    count = lax.axis_size(AXES)
    return lax.ppermute(block, AXES, [((i - distance) % count, i) for i in range(count)])


def project_kernel(*refs):
    blocks = (len(refs) - 3) // 2
    xs, weights, outs = refs[:blocks], refs[blocks : blocks + 3], refs[blocks + 3 :]
    for n, w_ref in enumerate(weights):
        for x_ref, out_ref in zip(xs, outs):
            recs, seq, width = x_ref.shape
            made = mm(x_ref[...].reshape(recs * seq, width), w_ref[...])
            out_ref[:, :, n * width : (n + 1) * width] = made.astype(jnp.bfloat16).reshape(recs, seq, width)


def project(blocks, weights):
    rows = sum(block.shape[0] * block.shape[1] for block in blocks)
    width = blocks[0].shape[2]
    return pl.pallas_call(
        project_kernel,
        out_shape=[jax.ShapeDtypeStruct(block.shape[:2] + (3 * width,), jnp.bfloat16) for block in blocks],
        in_specs=[VMEM] * (len(blocks) + 3),
        out_specs=[VMEM] * len(blocks),
        compiler_params=pltpu.CompilerParams(vmem_limit_bytes=18 << 20),
        cost_estimate=pl.CostEstimate(flops=6 * rows * width * width, bytes_accessed=14 << 20, transcendentals=0),
        name="project",
    )(*blocks, *weights)


def pairs_kernel(
    info_ref, own_ref, left_x, right_x, wq_ref, wk_ref, wv_ref, grads_ref, z_ref, loss_ref, win, sem, *, count
):
    _, seq, full = win.shape
    recs, width = own_ref.shape[0], full // 3
    rows = recs * seq
    copy = pltpu.make_async_copy(own_ref, win.at[pl.ds(recs, recs)], sem)
    copy.start()
    x = jnp.concatenate([left_x[...].reshape(rows, width), right_x[...].reshape(rows, width)], axis=0)
    for n, w_ref in enumerate((wq_ref, wk_ref, wv_ref)):
        made = mm(x, w_ref[...]).astype(jnp.bfloat16)
        at = slice(n * width, (n + 1) * width)
        win[:recs, :, at] = made[:rows].reshape(recs, seq, width)
        win[2 * recs :, :, at] = made[rows:].reshape(recs, seq, width)

    lane = lax.broadcasted_iota(jnp.int32, (seq, 128), 1)
    first = lane < 64
    row = lax.broadcasted_iota(jnp.int32, (2 * seq, 128), 0)
    col = lax.broadcasted_iota(jnp.int32, (2 * seq, 128), 1)
    ends = jnp.where((row < seq) == (col < 64), 1.0, 0.0).astype(jnp.bfloat16)
    zero = jnp.zeros((seq, 128), jnp.bfloat16)
    copy.wait()
    loss_ref[...] = jnp.zeros_like(loss_ref)

    def one_pair(p, _):
        a, b = info_ref[p], info_ref[count + p]
        jobs = []
        for i in range(width // 128):
            at = [slice(n * width + i * 128, n * width + (i + 1) * 128) for n in range(3)]
            qa, ka, va = (win[a, :, s] for s in at)
            qb, kb, vb = (win[b, :, s] for s in at)
            jobs.append((at, 0, count, qa, kb, vb))
            jobs.append((at, count, 0, qb, ka, va))
        qs = [
            jnp.concatenate([jnp.where(first, job[3], zero), jnp.where(first, zero, job[3])], axis=0) for job in jobs
        ]
        scores = [mm(job[4], q, NT) for job, q in zip(jobs, qs)]
        probs = []
        for s in scores:
            top = jnp.max(s, axis=0, keepdims=True)
            e = jnp.exp2((s - top) * (LOG2_E / 8.0))
            probs.append(e * (1.0 / jnp.sum(e, axis=0, keepdims=True)))
        mass = [mm(prob.astype(jnp.bfloat16), ends) for prob in probs]
        pooled = [
            jnp.sum(m * job[5].astype(jnp.float32), axis=0, keepdims=True) * (1.0 / seq) for m, job in zip(mass, jobs)
        ]
        z = jnp.zeros((1, 128), jnp.float32)
        for i in range(width // 128):
            z = z + pooled[2 * i] * pooled[2 * i + 1]
        z = 4.0 * jnp.sum(z)
        z_ref[p] = z
        c = info_ref[2 * count + p].astype(jnp.float32) * (1.0 / 256.0)
        y = info_ref[3 * count + p].astype(jnp.float32)
        z = jnp.full(loss_ref.shape, z, jnp.float32)
        loss_ref[...] += c * (jnp.maximum(z, 0.0) + jnp.log1p(jnp.exp(-jnp.abs(z))) - y * z)
        dps = [pooled[n ^ 1] * (4.0 / seq) for n in range(len(jobs))]
        ts = [
            mm((job[5].astype(jnp.float32) * (dp * 0.125)).astype(jnp.bfloat16), ends, NT)
            for dp, job in zip(dps, jobs)
        ]
        dss = []
        for prob, t in zip(probs, ts):
            r = jnp.sum(prob * t, axis=0, keepdims=True)
            dss.append((prob * (t - r)).astype(jnp.bfloat16))
        dks = [mm(ds, q) for ds, q in zip(dss, qs)]
        dqs = [mm(ds, job[4], TN) for ds, job in zip(dss, jobs)]
        for n, (at, qrow, krow, _, _, _) in enumerate(jobs):
            grads_ref[krow + p, :, at[2]] = (mass[n] * dps[n]).astype(jnp.bfloat16)
            grads_ref[krow + p, :, at[1]] = dks[n].astype(jnp.bfloat16)
            grads_ref[qrow + p, :, at[0]] = jnp.where(first, dqs[n][:seq], dqs[n][seq:]).astype(jnp.bfloat16)
        return 0

    lax.fori_loop(0, count, one_pair, 0)


def pairs(info, own, left_x, right_x, weights, count):
    recs, seq, full = own.shape
    return pl.pallas_call(
        functools.partial(pairs_kernel, count=count),
        out_shape=(
            jax.ShapeDtypeStruct((2 * count, seq, full), jnp.bfloat16),
            jax.ShapeDtypeStruct((count,), jnp.float32),
            jax.ShapeDtypeStruct((8, 128), jnp.float32),
        ),
        in_specs=[SMEM, ANY] + [VMEM] * 5,
        out_specs=(VMEM, SMEM, VMEM),
        scratch_shapes=[pltpu.VMEM((3 * recs, seq, full), jnp.bfloat16), pltpu.SemaphoreType.DMA],
        compiler_params=pltpu.CompilerParams(vmem_limit_bytes=28 << 20),
        cost_estimate=pl.CostEstimate(flops=12 << 30, bytes_accessed=12 << 20, transcendentals=2 << 20),
        name="pairs",
    )(info, own, left_x, right_x, *weights)


def terms_kernel(info_ref, z_ref, g_ref, wq_ref, wk_ref, wv_ref, left_ref, own_ref, right_ref, acc, *, count):
    _, seq, full = g_ref.shape
    width, recs, tile = full // 3, left_ref.shape[0], acc.shape[2]
    scales = []
    for p in range(count):
        z = jnp.full((8, 128), z_ref[p], jnp.float32)
        c = info_ref[2 * count + p].astype(jnp.float32) * (1.0 / 256.0)
        y = info_ref[3 * count + p].astype(jnp.float32)
        scales.append((seq * c * (jax.nn.sigmoid(z) - y))[0:1, 0:1])
    for start in range(0, left_ref.shape[2], tile):
        columns = slice(start, start + tile)
        made = None
        for n, w_ref in enumerate((wq_ref, wk_ref, wv_ref)):
            grads = g_ref[:, :, n * width : (n + 1) * width].reshape(2 * count * seq, width)
            part = mm(grads, w_ref[columns, :], NT)
            made = part if made is None else made + part
        acc[...] = jnp.zeros_like(acc)
        for n in range(2 * count):
            acc[info_ref[n]] += made[n * seq : (n + 1) * seq] * scales[n % count]
        for n, out in enumerate((left_ref, own_ref, right_ref)):
            out[:, :, columns] = acc[n * recs : (n + 1) * recs].astype(jnp.bfloat16)


def terms(info, z, grads, weights, recs, count):
    _, seq, full = grads.shape
    size = weights[0].shape[0]
    made = jax.ShapeDtypeStruct((recs, seq, size), jnp.bfloat16)
    return pl.pallas_call(
        functools.partial(terms_kernel, count=count),
        out_shape=(made, made, made),
        in_specs=[SMEM, SMEM] + [VMEM] * 4,
        out_specs=(VMEM,) * 3,
        scratch_shapes=[pltpu.VMEM((3 * recs, seq, 512), jnp.float32)],
        compiler_params=pltpu.CompilerParams(vmem_limit_bytes=18 << 20),
        cost_estimate=pl.CostEstimate(
            flops=4 * count * seq * full * size, bytes_accessed=12 << 20, transcendentals=0
        ),
        name="terms",
    )(info, z, grads, *weights)


def row_total(value):
    count = lax.axis_size(AXES)
    routes = [[(i, i - i % ROW + (i + k) % ROW) for i in range(count)] for k in range(1, ROW)]
    return sum([lax.ppermute(value, AXES, route) for route in routes], value)


def column_total(value):
    rows = lax.axis_size(AXES) // ROW
    groups = [[h * ROW + x for h in range(rows)] for x in range(ROW)]
    spread = jnp.broadcast_to(value[0:1], (rows, value.shape[1]))
    met = lax.all_to_all(spread, AXES, 0, 0, axis_index_groups=groups, tiled=True)
    return jnp.sum(met, axis=0)[0]


def on_device(records, w_query, w_key, w_value, pair_owner, pair_partner, confidence, labels):
    recs, seq, width = records.shape
    count = pair_owner.shape[0]
    devices = lax.axis_size(AXES)
    first_id = lax.axis_index(AXES) * recs
    weights = (w_query, w_key, w_value)

    left_records = from_behind(records, 1)
    right_records = from_behind(records, -1)
    own_info = jnp.concatenate(
        [pair_owner - first_id, jnp.mod(pair_partner - first_id, recs * devices), confidence, labels]
    )
    info = from_behind(own_info, 1)
    (own,) = project([records], weights)
    grads, z, loss = pairs(info, own, left_records, right_records, weights, count)

    z, loss = lax.optimization_barrier((z, loss))
    loss = row_total(loss)
    to_left, kept, to_right = terms(info, z, grads, weights, recs, count)
    to_left, to_right, loss = lax.optimization_barrier((to_left, to_right, loss))
    from_right, from_left = from_behind(to_left, -1), from_behind(to_right, 1)
    loss = column_total(loss) / (count * devices)
    record_grad = from_right.astype(jnp.float32) + kept.astype(jnp.float32) + from_left.astype(jnp.float32)
    return (loss, record_grad)


def solution(mesh):
    blocks = P(AXES, None, None)
    in_specs = (blocks, P(), P(), P(), P(AXES), P(AXES), P(AXES), P(AXES))
    return jax.shard_map(
        on_device, mesh=mesh, in_specs=in_specs, out_specs=(P(), blocks), check_vma=False
    )
```

```python
import functools

import jax
import jax.numpy as jnp
from jax import lax
from jax.experimental import pallas as pl
from jax.experimental.pallas import tpu as pltpu
from jax.sharding import PartitionSpec as P

AXES = ("dp", "mp")
ROW = 4
LAGS = (0, 2, 4, 6, 8, 10, 12, 14)
LOG2_E = 1.4426950408889634
NT = (((1,), (1,)), ((), ()))
TN = (((0,), (0,)), ((), ()))
VMEM = pl.BlockSpec(memory_space=pltpu.VMEM)
SMEM = pl.BlockSpec(memory_space=pltpu.SMEM)
ANY = pl.BlockSpec(memory_space=pl.ANY)


def mm(a, b, dims=(((1,), (0,)), ((), ()))):
    return lax.dot_general(a, b, dims, preferred_element_type=jnp.float32)


def from_behind(block, distance):
    count = lax.axis_size(AXES)
    return lax.ppermute(block, AXES, [((i - distance) % count, i) for i in range(count)])


def project_kernel(*refs):
    blocks = (len(refs) - 3) // 2
    xs, weights, outs = refs[:blocks], refs[blocks : blocks + 3], refs[blocks + 3 :]
    for n, w_ref in enumerate(weights):
        for x_ref, out_ref in zip(xs, outs):
            recs, seq, width = x_ref.shape
            made = mm(x_ref[...].reshape(recs * seq, width), w_ref[...])
            out_ref[:, :, n * width : (n + 1) * width] = made.astype(jnp.bfloat16).reshape(recs, seq, width)


def project(blocks, weights):
    rows = sum(block.shape[0] * block.shape[1] for block in blocks)
    width = blocks[0].shape[2]
    return pl.pallas_call(
        project_kernel,
        out_shape=[jax.ShapeDtypeStruct(block.shape[:2] + (3 * width,), jnp.bfloat16) for block in blocks],
        in_specs=[VMEM] * (len(blocks) + 3),
        out_specs=[VMEM] * len(blocks),
        compiler_params=pltpu.CompilerParams(vmem_limit_bytes=18 << 20),
        cost_estimate=pl.CostEstimate(flops=6 * rows * width * width, bytes_accessed=14 << 20, transcendentals=0),
        name="project",
    )(*blocks, *weights)


def pairs_kernel(
    info_ref, own_ref, left_x, right_x, wq_ref, wk_ref, wv_ref, to_left, kept, to_right, loss_ref, win, grads, scale, acc, sem,
    *, count, together
):
    _, seq, full = win.shape
    recs, width = own_ref.shape[0], full // 3
    rows = recs * seq
    weights = (wq_ref, wk_ref, wv_ref)
    copy = pltpu.make_async_copy(own_ref, win.at[pl.ds(recs, recs)], sem)
    copy.start()
    x = jnp.concatenate([left_x[...].reshape(rows, width), right_x[...].reshape(rows, width)], axis=0)
    for n, w_ref in enumerate(weights):
        made = mm(x, w_ref[...]).astype(jnp.bfloat16)
        at = slice(n * width, (n + 1) * width)
        win[:recs, :, at] = made[:rows].reshape(recs, seq, width)
        win[2 * recs :, :, at] = made[rows:].reshape(recs, seq, width)

    lane = lax.broadcasted_iota(jnp.int32, (seq, 128), 1)
    first = lane < 64
    row = lax.broadcasted_iota(jnp.int32, (2 * seq, 128), 0)
    col = lax.broadcasted_iota(jnp.int32, (2 * seq, 128), 1)
    ends = jnp.where((row < seq) == (col < 64), 1.0, 0.0).astype(jnp.bfloat16)
    ends_t = ends.astype(jnp.float32).T.astype(jnp.bfloat16)
    zero = jnp.zeros((seq, 128), jnp.bfloat16)
    copy.wait()
    loss_ref[...] = jnp.zeros_like(loss_ref)

    def some_pairs(i, _):
        blocks = width // 128
        jobs = []
        for k in range(together):
            p = i * together + k
            a, b = info_ref[p], info_ref[count + p]
            for j in range(blocks):
                jobs.append((k, j, a, b, p, count + p))
                jobs.append((k, j, b, a, count + p, p))
        qs, ks, probs, mass, pooled, dps, ts, dss, out = ({} for _ in range(9))

        def part(which, j):
            return slice(which * width + j * 128, which * width + (j + 1) * 128)

        def scores(n):
            _, j, mine, other, _, _ = jobs[n]
            q = win[mine, :, part(0, j)]
            qs[n] = jnp.concatenate([jnp.where(first, q, zero), jnp.where(first, zero, q)], axis=0)
            ks[n] = win[other, :, part(1, j)]
            probs[n] = mm(ks[n], qs[n], NT)

        def softmax(n):
            top = jnp.max(probs[n], axis=0, keepdims=True)
            e = jnp.exp2((probs[n] - top) * (LOG2_E / 8.0))
            probs[n] = e * (1.0 / jnp.sum(e, axis=0, keepdims=True))

        def masses(n):
            mass[n] = mm(probs[n].astype(jnp.bfloat16), ends)

        def pool(n):
            _, j, _, other, _, _ = jobs[n]
            v = win[other, :, part(2, j)].astype(jnp.float32)
            pooled[n] = jnp.sum(mass[n] * v, axis=0, keepdims=True) * (1.0 / seq)

        def t(n):
            _, j, _, other, _, _ = jobs[n]
            v = win[other, :, part(2, j)].astype(jnp.float32)
            dps[n] = pooled[n ^ 1] * (4.0 / seq)
            ts[n] = mm((v * (dps[n] * 0.125)).astype(jnp.bfloat16), ends_t)

        def ds(n):
            r = jnp.sum(probs[n] * ts[n], axis=0, keepdims=True)
            dss[n] = (probs[n] * (ts[n] - r)).astype(jnp.bfloat16)

        def products(n):
            out[n] = mm(dss[n], qs[n]), mm(dss[n], ks[n], TN)

        def store(n):
            _, j, _, _, mine, other = jobs[n]
            dk, dq = out[n]
            grads[other, :, part(2, j)] = (mass[n] * dps[n]).astype(jnp.bfloat16)
            grads[other, :, part(1, j)] = dk.astype(jnp.bfloat16)
            grads[mine, :, part(0, j)] = jnp.where(first, dq[:seq], dq[seq:]).astype(jnp.bfloat16)

        stages = list(zip((scores, softmax, masses, pool, t, ds, products, store), LAGS))
        for step in range(len(jobs) + LAGS[-1]):
            for stage, lag in stages:
                if 0 <= step - lag < len(jobs):
                    stage(step - lag)

        for k in range(together):
            p = i * together + k
            z = sum(pooled[n] * pooled[n + 1] for n in range(2 * blocks * k, 2 * blocks * (k + 1), 2))
            z = jnp.full((8, 128), 4.0 * jnp.sum(z), jnp.float32)
            c = info_ref[2 * count + p].astype(jnp.float32) * (1.0 / 256.0)
            y = info_ref[3 * count + p].astype(jnp.float32)
            loss_ref[...] += c * (jnp.maximum(z, 0.0) + jnp.log1p(jnp.exp(-jnp.abs(z))) - y * z)
            scale[p] = seq * c * (jax.nn.sigmoid(z) - y)
        return 0

    lax.fori_loop(0, count // together, some_pairs, 0)

    tile = acc.shape[2]
    for start in range(0, width, tile):
        columns = slice(start, start + tile)
        made = None
        for n, w_ref in enumerate(weights):
            part = grads[:, :, n * width : (n + 1) * width].reshape(2 * count * seq, width)
            part = mm(part, w_ref[columns, :], NT)
            made = part if made is None else made + part
        acc[...] = jnp.zeros_like(acc)
        for n in range(2 * count):
            acc[info_ref[n]] += made[n * seq : (n + 1) * seq] * scale[n % count, 0:1, 0:1]
        for n, out in enumerate((to_left, kept, to_right)):
            out[:, :, columns] = acc[n * recs : (n + 1) * recs].astype(jnp.bfloat16)


def pairs(info, own, left_x, right_x, weights, count):
    recs, seq, full = own.shape
    width = full // 3
    made = jax.ShapeDtypeStruct((recs, seq, width), jnp.bfloat16)
    return pl.pallas_call(
        functools.partial(pairs_kernel, count=count, together=1),
        out_shape=(made, made, made, jax.ShapeDtypeStruct((8, 128), jnp.float32)),
        in_specs=[SMEM, ANY] + [VMEM] * 5,
        out_specs=(VMEM,) * 4,
        scratch_shapes=[
            pltpu.VMEM((3 * recs, seq, full), jnp.bfloat16),
            pltpu.VMEM((2 * count, seq, full), jnp.bfloat16),
            pltpu.VMEM((count, 8, 128), jnp.float32),
            pltpu.VMEM((3 * recs, seq, 512), jnp.float32),
            pltpu.SemaphoreType.DMA,
        ],
        compiler_params=pltpu.CompilerParams(vmem_limit_bytes=34 << 20),
        cost_estimate=pl.CostEstimate(flops=20 << 30, bytes_accessed=12 << 20, transcendentals=2 << 20),
        name="pairs",
    )(info, own, left_x, right_x, *weights)


def row_total(value):
    count = lax.axis_size(AXES)
    routes = [[(i, i - i % ROW + (i + k) % ROW) for i in range(count)] for k in range(1, ROW)]
    return sum([lax.ppermute(value, AXES, route) for route in routes], value)


def column_total(value):
    rows = lax.axis_size(AXES) // ROW
    groups = [[h * ROW + x for h in range(rows)] for x in range(ROW)]
    spread = jnp.broadcast_to(value[0:1], (rows, value.shape[1]))
    met = lax.all_to_all(spread, AXES, 0, 0, axis_index_groups=groups, tiled=True)
    return jnp.sum(met, axis=0, keepdims=True)


def combine_kernel(a_ref, b_ref, c_ref, out_ref):
    i = pl.program_id(0)
    out_ref[0] = a_ref[i].astype(jnp.float32) + b_ref[i].astype(jnp.float32) + c_ref[i].astype(jnp.float32)


def combine(first, second, third):
    recs, seq, width = first.shape
    return pl.pallas_call(
        combine_kernel,
        grid=(recs,),
        out_shape=jax.ShapeDtypeStruct(first.shape, jnp.float32),
        in_specs=[VMEM] * 3,
        out_specs=pl.BlockSpec((1, seq, width), lambda i: (i, 0, 0)),
        compiler_params=pltpu.CompilerParams(vmem_limit_bytes=16 << 20),
        cost_estimate=pl.CostEstimate(flops=2 * first.size, bytes_accessed=4 * first.size, transcendentals=0),
        name="combine",
    )(first, second, third)


def on_device(records, w_query, w_key, w_value, pair_owner, pair_partner, confidence, labels):
    recs, seq, width = records.shape
    count = pair_owner.shape[0]
    devices = lax.axis_size(AXES)
    first_id = lax.axis_index(AXES) * recs
    weights = (w_query, w_key, w_value)

    left_records = from_behind(records, 1)
    right_records = from_behind(records, -1)
    own_info = jnp.concatenate(
        [pair_owner - first_id, jnp.mod(pair_partner - first_id, recs * devices), confidence, labels]
    )
    info = from_behind(own_info, 1)
    (own,) = project([records], weights)
    to_left, kept, to_right, loss = pairs(info, own, left_records, right_records, weights, count)
    from_right, from_left = from_behind(to_left, -1), from_behind(to_right, 1)
    loss = row_total(column_total(loss)) / (count * devices)
    record_grad = combine(from_right, kept, from_left)
    return (loss[0, 0], record_grad)


def solution(mesh):
    blocks = P(AXES, None, None)
    in_specs = (blocks, P(), P(), P(), P(AXES), P(AXES), P(AXES), P(AXES))
    return jax.shard_map(
        on_device, mesh=mesh, in_specs=in_specs, out_specs=(P(), blocks), check_vma=False
    )
```

```python
import functools

import jax
import jax.numpy as jnp
from jax import lax
from jax.experimental import pallas as pl
from jax.experimental.pallas import tpu as pltpu
from jax.sharding import PartitionSpec as P

AXES = ("dp", "mp")
ROW = 4
LAGS = (0, 2, 4, 6, 8, 10, 12, 14)
LOG2_E = 1.4426950408889634
NT = (((1,), (1,)), ((), ()))
TN = (((0,), (0,)), ((), ()))
VMEM = pl.BlockSpec(memory_space=pltpu.VMEM)
SMEM = pl.BlockSpec(memory_space=pltpu.SMEM)
ANY = pl.BlockSpec(memory_space=pl.ANY)


def mm(a, b, dims=(((1,), (0,)), ((), ()))):
    return lax.dot_general(a, b, dims, preferred_element_type=jnp.float32)


def from_behind(block, distance):
    count = lax.axis_size(AXES)
    return lax.ppermute(block, AXES, [((i - distance) % count, i) for i in range(count)])


def project_kernel(*refs):
    blocks = (len(refs) - 3) // 2
    xs, weights, outs = refs[:blocks], refs[blocks : blocks + 3], refs[blocks + 3 :]
    for n, w_ref in enumerate(weights):
        for x_ref, out_ref in zip(xs, outs):
            recs, seq, width = x_ref.shape
            made = mm(x_ref[...].reshape(recs * seq, width), w_ref[...])
            out_ref[:, :, n * width : (n + 1) * width] = made.astype(jnp.bfloat16).reshape(recs, seq, width)


def project(blocks, weights):
    rows = sum(block.shape[0] * block.shape[1] for block in blocks)
    width = blocks[0].shape[2]
    return pl.pallas_call(
        project_kernel,
        out_shape=[jax.ShapeDtypeStruct(block.shape[:2] + (3 * width,), jnp.bfloat16) for block in blocks],
        in_specs=[VMEM] * (len(blocks) + 3),
        out_specs=[VMEM] * len(blocks),
        compiler_params=pltpu.CompilerParams(vmem_limit_bytes=18 << 20),
        cost_estimate=pl.CostEstimate(flops=6 * rows * width * width, bytes_accessed=14 << 20, transcendentals=0),
        name="project",
    )(*blocks, *weights)


def pairs_kernel(
    info_ref, own_ref, left_x, right_x, wq_ref, wk_ref, wv_ref, to_left, kept, to_right, loss_ref, win, grads, scale, acc, sem,
    *, count, together
):
    _, seq, full = win.shape
    recs, width = own_ref.shape[0], full // 3
    rows = recs * seq
    weights = (wq_ref, wk_ref, wv_ref)
    copy = pltpu.make_async_copy(own_ref, win.at[pl.ds(recs, recs)], sem)
    copy.start()
    x = jnp.concatenate([left_x[...].reshape(rows, width), right_x[...].reshape(rows, width)], axis=0)
    for n, w_ref in enumerate(weights):
        made = mm(x, w_ref[...]).astype(jnp.bfloat16)
        at = slice(n * width, (n + 1) * width)
        win[:recs, :, at] = made[:rows].reshape(recs, seq, width)
        win[2 * recs :, :, at] = made[rows:].reshape(recs, seq, width)

    lane = lax.broadcasted_iota(jnp.int32, (seq, 128), 1)
    first = lane < 64
    row = lax.broadcasted_iota(jnp.int32, (2 * seq, 128), 0)
    col = lax.broadcasted_iota(jnp.int32, (2 * seq, 128), 1)
    ends = jnp.where((row < seq) == (col < 64), 1.0, 0.0).astype(jnp.bfloat16)
    ends_t = ends.astype(jnp.float32).T.astype(jnp.bfloat16)
    zero = jnp.zeros((seq, 128), jnp.bfloat16)
    copy.wait()
    loss_ref[...] = jnp.zeros_like(loss_ref)

    def some_pairs(i, _):
        blocks = width // 128
        jobs = []
        for k in range(together):
            p = i * together + k
            a, b = info_ref[p], info_ref[count + p]
            for j in range(blocks):
                jobs.append((k, j, a, b, p, count + p))
                jobs.append((k, j, b, a, count + p, p))
        qs, ks, probs, mass, pooled, dps, ts, dss, out = ({} for _ in range(9))

        def part(which, j):
            return slice(which * width + j * 128, which * width + (j + 1) * 128)

        def scores(n):
            _, j, mine, other, _, _ = jobs[n]
            q = win[mine, :, part(0, j)]
            qs[n] = jnp.concatenate([jnp.where(first, q, zero), jnp.where(first, zero, q)], axis=0)
            ks[n] = win[other, :, part(1, j)]
            probs[n] = mm(ks[n], qs[n], NT)

        def softmax(n):
            top = jnp.max(probs[n], axis=0, keepdims=True)
            e = jnp.exp2((probs[n] - top) * (LOG2_E / 8.0))
            probs[n] = e * (1.0 / jnp.sum(e, axis=0, keepdims=True))

        def masses(n):
            mass[n] = mm(probs[n].astype(jnp.bfloat16), ends)

        def pool(n):
            _, j, _, other, _, _ = jobs[n]
            v = win[other, :, part(2, j)].astype(jnp.float32)
            pooled[n] = jnp.sum(mass[n] * v, axis=0, keepdims=True) * (1.0 / seq)

        def t(n):
            _, j, _, other, _, _ = jobs[n]
            v = win[other, :, part(2, j)].astype(jnp.float32)
            dps[n] = pooled[n ^ 1] * (4.0 / seq)
            ts[n] = mm((v * (dps[n] * 0.125)).astype(jnp.bfloat16), ends_t)

        def ds(n):
            r = jnp.sum(probs[n] * ts[n], axis=0, keepdims=True)
            dss[n] = (probs[n] * (ts[n] - r)).astype(jnp.bfloat16)

        def products(n):
            out[n] = mm(dss[n], qs[n]), mm(dss[n], ks[n], TN)

        def store(n):
            _, j, _, _, mine, other = jobs[n]
            dk, dq = out[n]
            grads[other, :, part(2, j)] = (mass[n] * dps[n]).astype(jnp.bfloat16)
            grads[other, :, part(1, j)] = dk.astype(jnp.bfloat16)
            grads[mine, :, part(0, j)] = jnp.where(first, dq[:seq], dq[seq:]).astype(jnp.bfloat16)

        stages = list(zip((scores, softmax, masses, pool, t, ds, products, store), LAGS))
        for step in range(len(jobs) + LAGS[-1]):
            for stage, lag in stages:
                if 0 <= step - lag < len(jobs):
                    stage(step - lag)

        for k in range(together):
            p = i * together + k
            z = sum(pooled[n] * pooled[n + 1] for n in range(2 * blocks * k, 2 * blocks * (k + 1), 2))
            z = jnp.full((8, 128), 4.0 * jnp.sum(z), jnp.float32)
            c = info_ref[2 * count + p].astype(jnp.float32) * (1.0 / 256.0)
            y = info_ref[3 * count + p].astype(jnp.float32)
            loss_ref[...] += c * (jnp.maximum(z, 0.0) + jnp.log1p(jnp.exp(-jnp.abs(z))) - y * z)
            scale[p] = seq * c * (jax.nn.sigmoid(z) - y)
        return 0

    lax.fori_loop(0, count // together, some_pairs, 0)

    tile = acc.shape[2]
    for start in range(0, width, tile):
        columns = slice(start, start + tile)
        made = None
        for n, w_ref in enumerate(weights):
            part = grads[:, :, n * width : (n + 1) * width].reshape(2 * count * seq, width)
            part = mm(part, w_ref[columns, :], NT)
            made = part if made is None else made + part
        acc[...] = jnp.zeros_like(acc)
        for n in range(2 * count):
            acc[info_ref[n]] += made[n * seq : (n + 1) * seq] * scale[n % count, 0:1, 0:1]
        for n, out in enumerate((to_left, kept, to_right)):
            out[:, :, columns] = acc[n * recs : (n + 1) * recs].astype(jnp.bfloat16)


def pairs(info, own, left_x, right_x, weights, count):
    recs, seq, full = own.shape
    width = full // 3
    made = jax.ShapeDtypeStruct((recs, seq, width), jnp.bfloat16)
    return pl.pallas_call(
        functools.partial(pairs_kernel, count=count, together=2),
        out_shape=(made, made, made, jax.ShapeDtypeStruct((8, 128), jnp.float32)),
        in_specs=[SMEM, ANY] + [VMEM] * 5,
        out_specs=(VMEM,) * 4,
        scratch_shapes=[
            pltpu.VMEM((3 * recs, seq, full), jnp.bfloat16),
            pltpu.VMEM((2 * count, seq, full), jnp.bfloat16),
            pltpu.VMEM((count, 8, 128), jnp.float32),
            pltpu.VMEM((3 * recs, seq, 512), jnp.float32),
            pltpu.SemaphoreType.DMA,
        ],
        compiler_params=pltpu.CompilerParams(vmem_limit_bytes=34 << 20),
        cost_estimate=pl.CostEstimate(flops=20 << 30, bytes_accessed=12 << 20, transcendentals=2 << 20),
        name="pairs",
    )(info, own, left_x, right_x, *weights)


def row_met(value):
    count = lax.axis_size(AXES)
    routes = [[(i, i - i % ROW + (i + k) % ROW) for i in range(count)] for k in range(1, ROW)]
    return [lax.ppermute(value, AXES, route) for route in routes]


def column_total(value):
    rows = lax.axis_size(AXES) // ROW
    groups = [[h * ROW + x for h in range(rows)] for x in range(ROW)]
    spread = jnp.broadcast_to(value[0:1], (rows, value.shape[1]))
    met = lax.all_to_all(spread, AXES, 0, 0, axis_index_groups=groups, tiled=True)
    return jnp.sum(met, axis=0, keepdims=True)


def combine_kernel(a_ref, b_ref, c_ref, out_ref):
    i = pl.program_id(0)
    out_ref[0] = a_ref[i].astype(jnp.float32) + b_ref[i].astype(jnp.float32) + c_ref[i].astype(jnp.float32)


def combine(first, second, third):
    recs, seq, width = first.shape
    return pl.pallas_call(
        combine_kernel,
        grid=(recs,),
        out_shape=jax.ShapeDtypeStruct(first.shape, jnp.float32),
        in_specs=[VMEM] * 3,
        out_specs=pl.BlockSpec((1, seq, width), lambda i: (i, 0, 0)),
        compiler_params=pltpu.CompilerParams(vmem_limit_bytes=16 << 20),
        cost_estimate=pl.CostEstimate(flops=2 * first.size, bytes_accessed=4 * first.size, transcendentals=0),
        name="combine",
    )(first, second, third)


def on_device(records, w_query, w_key, w_value, pair_owner, pair_partner, confidence, labels):
    recs, seq, width = records.shape
    count = pair_owner.shape[0]
    devices = lax.axis_size(AXES)
    first_id = lax.axis_index(AXES) * recs
    weights = (w_query, w_key, w_value)

    left_records = from_behind(records, 1)
    right_records = from_behind(records, -1)
    own_info = jnp.concatenate(
        [pair_owner - first_id, jnp.mod(pair_partner - first_id, recs * devices), confidence, labels]
    )
    info = from_behind(own_info, 1)
    (own,) = project([records], weights)
    to_left, kept, to_right, loss = pairs(info, own, left_records, right_records, weights, count)
    from_right, from_left = from_behind(to_left, -1), from_behind(to_right, 1)
    loss = column_total(loss)
    met = row_met(loss)
    record_grad, loss = lax.optimization_barrier((combine(from_right, kept, from_left), loss))
    loss = sum(met, loss) / (count * devices)
    return (loss[0, 0], record_grad)


def solution(mesh):
    blocks = P(AXES, None, None)
    in_specs = (blocks, P(), P(), P(), P(AXES), P(AXES), P(AXES), P(AXES))
    return jax.shard_map(
        on_device, mesh=mesh, in_specs=in_specs, out_specs=(P(), blocks), check_vma=False
    )
```

```python
import functools

import jax
import jax.numpy as jnp
from jax import lax
from jax.experimental import pallas as pl
from jax.experimental.pallas import tpu as pltpu
from jax.sharding import PartitionSpec as P

AXES = ("dp", "mp")
ROW = 4
LAGS = (0, 2, 4, 6, 8, 10, 12, 14)
LOG2_E = 1.4426950408889634
NT = (((1,), (1,)), ((), ()))
TN = (((0,), (0,)), ((), ()))
VMEM = pl.BlockSpec(memory_space=pltpu.VMEM)
SMEM = pl.BlockSpec(memory_space=pltpu.SMEM)
ANY = pl.BlockSpec(memory_space=pl.ANY)


def mm(a, b, dims=(((1,), (0,)), ((), ()))):
    return lax.dot_general(a, b, dims, preferred_element_type=jnp.float32)


def from_behind(block, distance):
    count = lax.axis_size(AXES)
    return lax.ppermute(block, AXES, [((i - distance) % count, i) for i in range(count)])


def project_kernel(*refs):
    blocks = (len(refs) - 3) // 2
    xs, weights, outs = refs[:blocks], refs[blocks : blocks + 3], refs[blocks + 3 :]
    for n, w_ref in enumerate(weights):
        for x_ref, out_ref in zip(xs, outs):
            recs, seq, width = x_ref.shape
            made = mm(x_ref[...].reshape(recs * seq, width), w_ref[...])
            out_ref[:, :, n * width : (n + 1) * width] = made.astype(jnp.bfloat16).reshape(recs, seq, width)


def project(blocks, weights):
    rows = sum(block.shape[0] * block.shape[1] for block in blocks)
    width = blocks[0].shape[2]
    return pl.pallas_call(
        project_kernel,
        out_shape=[jax.ShapeDtypeStruct(block.shape[:2] + (3 * width,), jnp.bfloat16) for block in blocks],
        in_specs=[VMEM] * (len(blocks) + 3),
        out_specs=[VMEM] * len(blocks),
        compiler_params=pltpu.CompilerParams(vmem_limit_bytes=18 << 20),
        cost_estimate=pl.CostEstimate(flops=6 * rows * width * width, bytes_accessed=14 << 20, transcendentals=0),
        name="project",
    )(*blocks, *weights)


def pairs_kernel(
    info_ref, own_ref, left_x, right_x, wq_ref, wk_ref, wv_ref, to_left, kept, to_right, loss_ref, win, grads, scale, acc, sem,
    *, count, together
):
    _, seq, full = win.shape
    recs, width = own_ref.shape[0], full // 3
    rows = recs * seq
    weights = (wq_ref, wk_ref, wv_ref)
    copy = pltpu.make_async_copy(own_ref, win.at[pl.ds(recs, recs)], sem)
    copy.start()
    x = jnp.concatenate([left_x[...].reshape(rows, width), right_x[...].reshape(rows, width)], axis=0)
    for n, w_ref in enumerate(weights):
        made = mm(x, w_ref[...]).astype(jnp.bfloat16)
        at = slice(n * width, (n + 1) * width)
        win[:recs, :, at] = made[:rows].reshape(recs, seq, width)
        win[2 * recs :, :, at] = made[rows:].reshape(recs, seq, width)

    lane = lax.broadcasted_iota(jnp.int32, (seq, 128), 1)
    first = lane < 64
    row = lax.broadcasted_iota(jnp.int32, (2 * seq, 128), 0)
    col = lax.broadcasted_iota(jnp.int32, (2 * seq, 128), 1)
    ends = jnp.where((row < seq) == (col < 64), 1.0, 0.0).astype(jnp.bfloat16)
    ends_t = ends.astype(jnp.float32).T.astype(jnp.bfloat16)
    zero = jnp.zeros((seq, 128), jnp.bfloat16)
    copy.wait()
    loss_ref[...] = jnp.zeros_like(loss_ref)

    def some_pairs(i, _):
        blocks = width // 128
        jobs = []
        for k in range(together):
            p = i * together + k
            a, b = info_ref[p], info_ref[count + p]
            for j in range(blocks):
                jobs.append((k, j, a, b, p, count + p))
                jobs.append((k, j, b, a, count + p, p))
        qs, ks, probs, mass, pooled, dps, ts, dss, out = ({} for _ in range(9))

        def part(which, j):
            return slice(which * width + j * 128, which * width + (j + 1) * 128)

        def scores(n):
            _, j, mine, other, _, _ = jobs[n]
            q = win[mine, :, part(0, j)]
            qs[n] = jnp.concatenate([jnp.where(first, q, zero), jnp.where(first, zero, q)], axis=0)
            ks[n] = win[other, :, part(1, j)]
            probs[n] = mm(ks[n], qs[n], NT)

        def softmax(n):
            top = jnp.max(probs[n], axis=0, keepdims=True)
            e = jnp.exp2((probs[n] - top) * (LOG2_E / 8.0))
            probs[n] = e * (1.0 / jnp.sum(e, axis=0, keepdims=True))

        def masses(n):
            mass[n] = mm(probs[n].astype(jnp.bfloat16), ends)

        def pool(n):
            _, j, _, other, _, _ = jobs[n]
            v = win[other, :, part(2, j)].astype(jnp.float32)
            pooled[n] = jnp.sum(mass[n] * v, axis=0, keepdims=True) * (1.0 / seq)

        def t(n):
            _, j, _, other, _, _ = jobs[n]
            v = win[other, :, part(2, j)].astype(jnp.float32)
            dps[n] = pooled[n ^ 1] * (4.0 / seq)
            ts[n] = mm((v * (dps[n] * 0.125)).astype(jnp.bfloat16), ends_t)

        def ds(n):
            r = jnp.sum(probs[n] * ts[n], axis=0, keepdims=True)
            dss[n] = (probs[n] * (ts[n] - r)).astype(jnp.bfloat16)

        def products(n):
            out[n] = mm(dss[n], qs[n]), mm(dss[n], ks[n], TN)

        def store(n):
            _, j, _, _, mine, other = jobs[n]
            dk, dq = out[n]
            grads[other, :, part(2, j)] = (mass[n] * dps[n]).astype(jnp.bfloat16)
            grads[other, :, part(1, j)] = dk.astype(jnp.bfloat16)
            grads[mine, :, part(0, j)] = jnp.where(first, dq[:seq], dq[seq:]).astype(jnp.bfloat16)

        stages = list(zip((scores, softmax, masses, pool, t, ds, products, store), LAGS))
        for step in range(len(jobs) + LAGS[-1]):
            for stage, lag in stages:
                if 0 <= step - lag < len(jobs):
                    stage(step - lag)

        for k in range(together):
            p = i * together + k
            z = sum(pooled[n] * pooled[n + 1] for n in range(2 * blocks * k, 2 * blocks * (k + 1), 2))
            z = jnp.full((8, 128), 4.0 * jnp.sum(z), jnp.float32)
            c = info_ref[2 * count + p].astype(jnp.float32) * (1.0 / 256.0)
            y = info_ref[3 * count + p].astype(jnp.float32)
            loss_ref[...] += c * (jnp.maximum(z, 0.0) + jnp.log1p(jnp.exp(-jnp.abs(z))) - y * z)
            scale[p] = seq * c * (jax.nn.sigmoid(z) - y)
        return 0

    lax.fori_loop(0, count // together, some_pairs, 0)

    tile = acc.shape[2]
    for start in range(0, width, tile):
        columns = slice(start, start + tile)
        made = None
        for n, w_ref in enumerate(weights):
            part = grads[:, :, n * width : (n + 1) * width].reshape(2 * count * seq, width)
            part = mm(part, w_ref[columns, :], NT)
            made = part if made is None else made + part
        acc[...] = jnp.zeros_like(acc)
        for n in range(2 * count):
            acc[info_ref[n]] += made[n * seq : (n + 1) * seq] * scale[n % count, 0:1, 0:1]
        for n, out in enumerate((to_left, kept, to_right)):
            out[:, :, columns] = acc[n * recs : (n + 1) * recs].astype(jnp.bfloat16)


def pairs(info, own, left_x, right_x, weights, count):
    recs, seq, full = own.shape
    width = full // 3
    made = jax.ShapeDtypeStruct((recs, seq, width), jnp.bfloat16)
    return pl.pallas_call(
        functools.partial(pairs_kernel, count=count, together=4),
        out_shape=(made, made, made, jax.ShapeDtypeStruct((8, 128), jnp.float32)),
        in_specs=[SMEM, ANY] + [VMEM] * 5,
        out_specs=(VMEM,) * 4,
        scratch_shapes=[
            pltpu.VMEM((3 * recs, seq, full), jnp.bfloat16),
            pltpu.VMEM((2 * count, seq, full), jnp.bfloat16),
            pltpu.VMEM((count, 8, 128), jnp.float32),
            pltpu.VMEM((3 * recs, seq, 512), jnp.float32),
            pltpu.SemaphoreType.DMA,
        ],
        compiler_params=pltpu.CompilerParams(vmem_limit_bytes=34 << 20),
        cost_estimate=pl.CostEstimate(flops=20 << 30, bytes_accessed=12 << 20, transcendentals=2 << 20),
        name="pairs",
    )(info, own, left_x, right_x, *weights)


def row_met(value):
    count = lax.axis_size(AXES)
    routes = [[(i, i - i % ROW + (i + k) % ROW) for i in range(count)] for k in range(1, ROW)]
    return [lax.ppermute(value, AXES, route) for route in routes]


def column_total(value):
    rows = lax.axis_size(AXES) // ROW
    groups = [[h * ROW + x for h in range(rows)] for x in range(ROW)]
    spread = jnp.broadcast_to(value[0:1], (rows, value.shape[1]))
    met = lax.all_to_all(spread, AXES, 0, 0, axis_index_groups=groups, tiled=True)
    return jnp.sum(met, axis=0, keepdims=True)


def combine_kernel(a_ref, b_ref, c_ref, out_ref, made, sems):
    parts = sems.shape[0]
    recs, seq, _ = made.shape
    rows = recs * seq // parts
    leaving = []
    for n in range(parts):
        at = (n * rows // seq, slice(n * rows % seq, n * rows % seq + rows))
        made[at] = a_ref[at].astype(jnp.float32) + b_ref[at].astype(jnp.float32) + c_ref[at].astype(jnp.float32)
        leaving.append(pltpu.make_async_copy(made.at[at], out_ref.at[at], sems.at[n]))
        leaving[-1].start()
    for copy in leaving:
        copy.wait()


def combine(first, second, third):
    return pl.pallas_call(
        combine_kernel,
        out_shape=jax.ShapeDtypeStruct(first.shape, jnp.float32),
        in_specs=[VMEM] * 3,
        out_specs=pl.BlockSpec(memory_space=pltpu.HBM),
        scratch_shapes=[pltpu.VMEM(first.shape, jnp.float32), pltpu.SemaphoreType.DMA((4,))],
        compiler_params=pltpu.CompilerParams(vmem_limit_bytes=16 << 20),
        cost_estimate=pl.CostEstimate(flops=2 * first.size, bytes_accessed=4 * first.size, transcendentals=0),
        name="combine",
    )(first, second, third)


def on_device(records, w_query, w_key, w_value, pair_owner, pair_partner, confidence, labels):
    recs, seq, width = records.shape
    count = pair_owner.shape[0]
    devices = lax.axis_size(AXES)
    first_id = lax.axis_index(AXES) * recs
    weights = (w_query, w_key, w_value)

    left_records = from_behind(records, 1)
    right_records = from_behind(records, -1)
    own_info = jnp.concatenate(
        [pair_owner - first_id, jnp.mod(pair_partner - first_id, recs * devices), confidence, labels]
    )
    info = from_behind(own_info, 1)
    (own,) = project([records], weights)
    to_left, kept, to_right, loss = pairs(info, own, left_records, right_records, weights, count)
    from_right, from_left = from_behind(to_left, -1), from_behind(to_right, 1)
    loss = column_total(loss)
    met = row_met(loss)
    record_grad, loss = lax.optimization_barrier((combine(from_right, kept, from_left), loss))
    loss = sum(met, loss) / (count * devices)
    return (loss[0, 0], record_grad)


def solution(mesh):
    blocks = P(AXES, None, None)
    in_specs = (blocks, P(), P(), P(), P(AXES), P(AXES), P(AXES), P(AXES))
    return jax.shard_map(
        on_device, mesh=mesh, in_specs=in_specs, out_specs=(P(), blocks), check_vma=False
    )
```

```python
import functools

import jax
import jax.numpy as jnp
from jax import lax
from jax.experimental import pallas as pl
from jax.experimental.pallas import tpu as pltpu
from jax.sharding import PartitionSpec as P

AXES = ("dp", "mp")
ROW = 4
LAGS = (0, 3, 6, 9, 12, 15, 18, 21)
LOG2_E = 1.4426950408889634
NT = (((1,), (1,)), ((), ()))
TN = (((0,), (0,)), ((), ()))
VMEM = pl.BlockSpec(memory_space=pltpu.VMEM)
SMEM = pl.BlockSpec(memory_space=pltpu.SMEM)
ANY = pl.BlockSpec(memory_space=pl.ANY)


def mm(a, b, dims=(((1,), (0,)), ((), ()))):
    return lax.dot_general(a, b, dims, preferred_element_type=jnp.float32)


def from_behind(block, distance):
    count = lax.axis_size(AXES)
    return lax.ppermute(block, AXES, [((i - distance) % count, i) for i in range(count)])


def project_kernel(*refs):
    blocks = (len(refs) - 3) // 2
    xs, weights, outs = refs[:blocks], refs[blocks : blocks + 3], refs[blocks + 3 :]
    for n, w_ref in enumerate(weights):
        for x_ref, out_ref in zip(xs, outs):
            recs, seq, width = x_ref.shape
            made = mm(x_ref[...].reshape(recs * seq, width), w_ref[...])
            out_ref[:, :, n * width : (n + 1) * width] = made.astype(jnp.bfloat16).reshape(recs, seq, width)


def project(blocks, weights):
    rows = sum(block.shape[0] * block.shape[1] for block in blocks)
    width = blocks[0].shape[2]
    return pl.pallas_call(
        project_kernel,
        out_shape=[jax.ShapeDtypeStruct(block.shape[:2] + (3 * width,), jnp.bfloat16) for block in blocks],
        in_specs=[VMEM] * (len(blocks) + 3),
        out_specs=[VMEM] * len(blocks),
        compiler_params=pltpu.CompilerParams(vmem_limit_bytes=18 << 20),
        cost_estimate=pl.CostEstimate(flops=6 * rows * width * width, bytes_accessed=14 << 20, transcendentals=0),
        name="project",
    )(*blocks, *weights)


def pairs_kernel(
    info_ref, own_ref, left_x, right_x, wq_ref, wk_ref, wv_ref, to_left, kept, to_right, loss_ref, win, grads, scale, acc, sem,
    *, count, together
):
    _, seq, full = win.shape
    recs, width = own_ref.shape[0], full // 3
    rows = recs * seq
    weights = (wq_ref, wk_ref, wv_ref)
    copy = pltpu.make_async_copy(own_ref, win.at[pl.ds(recs, recs)], sem)
    copy.start()
    x = jnp.concatenate([left_x[...].reshape(rows, width), right_x[...].reshape(rows, width)], axis=0)
    for n, w_ref in enumerate(weights):
        made = mm(x, w_ref[...]).astype(jnp.bfloat16)
        at = slice(n * width, (n + 1) * width)
        win[:recs, :, at] = made[:rows].reshape(recs, seq, width)
        win[2 * recs :, :, at] = made[rows:].reshape(recs, seq, width)

    lane = lax.broadcasted_iota(jnp.int32, (seq, 128), 1)
    first = lane < 64
    row = lax.broadcasted_iota(jnp.int32, (2 * seq, 128), 0)
    col = lax.broadcasted_iota(jnp.int32, (2 * seq, 128), 1)
    ends = jnp.where((row < seq) == (col < 64), 1.0, 0.0).astype(jnp.bfloat16)
    ends_t = ends.astype(jnp.float32).T.astype(jnp.bfloat16)
    zero = jnp.zeros((seq, 128), jnp.bfloat16)
    copy.wait()
    loss_ref[...] = jnp.zeros_like(loss_ref)

    def some_pairs(i, _):
        blocks = width // 128
        jobs = []
        for k in range(together):
            p = i * together + k
            a, b = info_ref[p], info_ref[count + p]
            for j in range(blocks):
                jobs.append((k, j, a, b, p, count + p))
                jobs.append((k, j, b, a, count + p, p))
        qs, ks, probs, mass, pooled, dps, ts, dss, out = ({} for _ in range(9))

        def part(which, j):
            return slice(which * width + j * 128, which * width + (j + 1) * 128)

        def scores(n):
            _, j, mine, other, _, _ = jobs[n]
            q = win[mine, :, part(0, j)]
            qs[n] = jnp.concatenate([jnp.where(first, q, zero), jnp.where(first, zero, q)], axis=0)
            ks[n] = win[other, :, part(1, j)]
            probs[n] = mm(ks[n], qs[n], NT)

        def softmax(n):
            top = jnp.max(probs[n], axis=0, keepdims=True)
            e = jnp.exp2((probs[n] - top) * (LOG2_E / 8.0))
            probs[n] = e * (1.0 / jnp.sum(e, axis=0, keepdims=True))

        def masses(n):
            mass[n] = mm(probs[n].astype(jnp.bfloat16), ends)

        def pool(n):
            _, j, _, other, _, _ = jobs[n]
            v = win[other, :, part(2, j)].astype(jnp.float32)
            pooled[n] = jnp.sum(mass[n] * v, axis=0, keepdims=True) * (1.0 / seq)

        def t(n):
            _, j, _, other, _, _ = jobs[n]
            v = win[other, :, part(2, j)].astype(jnp.float32)
            dps[n] = pooled[n ^ 1] * (4.0 / seq)
            ts[n] = mm((v * (dps[n] * 0.125)).astype(jnp.bfloat16), ends_t)

        def ds(n):
            r = jnp.sum(probs[n] * ts[n], axis=0, keepdims=True)
            dss[n] = (probs[n] * (ts[n] - r)).astype(jnp.bfloat16)

        def products(n):
            out[n] = mm(dss[n], qs[n]), mm(dss[n], ks[n], TN)

        def store(n):
            _, j, _, _, mine, other = jobs[n]
            dk, dq = out[n]
            grads[other, :, part(2, j)] = (mass[n] * dps[n]).astype(jnp.bfloat16)
            grads[other, :, part(1, j)] = dk.astype(jnp.bfloat16)
            grads[mine, :, part(0, j)] = jnp.where(first, dq[:seq], dq[seq:]).astype(jnp.bfloat16)

        stages = list(zip((scores, softmax, masses, pool, t, ds, products, store), LAGS))
        for step in range(len(jobs) + LAGS[-1]):
            for stage, lag in stages:
                if 0 <= step - lag < len(jobs):
                    stage(step - lag)

        for k in range(together):
            p = i * together + k
            z = sum(pooled[n] * pooled[n + 1] for n in range(2 * blocks * k, 2 * blocks * (k + 1), 2))
            z = jnp.full((8, 128), 4.0 * jnp.sum(z), jnp.float32)
            c = info_ref[2 * count + p].astype(jnp.float32) * (1.0 / 256.0)
            y = info_ref[3 * count + p].astype(jnp.float32)
            loss_ref[...] += c * (jnp.maximum(z, 0.0) + jnp.log1p(jnp.exp(-jnp.abs(z))) - y * z)
            scale[p] = seq * c * (jax.nn.sigmoid(z) - y)
        return 0

    lax.fori_loop(0, count // together, some_pairs, 0)

    tile = acc.shape[2]
    for start in range(0, width, tile):
        columns = slice(start, start + tile)
        made = None
        for n, w_ref in enumerate(weights):
            part = grads[:, :, n * width : (n + 1) * width].reshape(2 * count * seq, width)
            part = mm(part, w_ref[columns, :], NT)
            made = part if made is None else made + part
        acc[...] = jnp.zeros_like(acc)
        for n in range(2 * count):
            acc[info_ref[n]] += made[n * seq : (n + 1) * seq] * scale[n % count, 0:1, 0:1]
        for n, out in enumerate((to_left, kept, to_right)):
            out[:, :, columns] = acc[n * recs : (n + 1) * recs].astype(jnp.bfloat16)


def pairs(info, own, left_x, right_x, weights, count):
    recs, seq, full = own.shape
    width = full // 3
    made = jax.ShapeDtypeStruct((recs, seq, width), jnp.bfloat16)
    return pl.pallas_call(
        functools.partial(pairs_kernel, count=count, together=4),
        out_shape=(made, made, made, jax.ShapeDtypeStruct((8, 128), jnp.float32)),
        in_specs=[SMEM, ANY] + [VMEM] * 5,
        out_specs=(VMEM,) * 4,
        scratch_shapes=[
            pltpu.VMEM((3 * recs, seq, full), jnp.bfloat16),
            pltpu.VMEM((2 * count, seq, full), jnp.bfloat16),
            pltpu.VMEM((count, 8, 128), jnp.float32),
            pltpu.VMEM((3 * recs, seq, 512), jnp.float32),
            pltpu.SemaphoreType.DMA,
        ],
        compiler_params=pltpu.CompilerParams(vmem_limit_bytes=34 << 20),
        cost_estimate=pl.CostEstimate(flops=20 << 30, bytes_accessed=12 << 20, transcendentals=2 << 20),
        name="pairs",
    )(info, own, left_x, right_x, *weights)


def row_met(value):
    count = lax.axis_size(AXES)
    routes = [[(i, i - i % ROW + (i + k) % ROW) for i in range(count)] for k in range(1, ROW)]
    return [lax.ppermute(value, AXES, route) for route in routes]


def column_total(value):
    rows = lax.axis_size(AXES) // ROW
    groups = [[h * ROW + x for h in range(rows)] for x in range(ROW)]
    spread = jnp.broadcast_to(value[0:1], (rows, value.shape[1]))
    met = lax.all_to_all(spread, AXES, 0, 0, axis_index_groups=groups, tiled=True)
    return jnp.sum(met, axis=0, keepdims=True)


def combine_kernel(a_ref, b_ref, c_ref, out_ref, made, sems):
    parts = sems.shape[0]
    recs, seq, _ = made.shape
    rows = recs * seq // parts
    leaving = []
    for n in range(parts):
        at = (n * rows // seq, slice(n * rows % seq, n * rows % seq + rows))
        made[at] = a_ref[at].astype(jnp.float32) + b_ref[at].astype(jnp.float32) + c_ref[at].astype(jnp.float32)
        leaving.append(pltpu.make_async_copy(made.at[at], out_ref.at[at], sems.at[n]))
        leaving[-1].start()
    for copy in leaving:
        copy.wait()


def combine(first, second, third):
    return pl.pallas_call(
        combine_kernel,
        out_shape=jax.ShapeDtypeStruct(first.shape, jnp.float32),
        in_specs=[VMEM] * 3,
        out_specs=pl.BlockSpec(memory_space=pltpu.HBM),
        scratch_shapes=[pltpu.VMEM(first.shape, jnp.float32), pltpu.SemaphoreType.DMA((4,))],
        compiler_params=pltpu.CompilerParams(vmem_limit_bytes=16 << 20),
        cost_estimate=pl.CostEstimate(flops=2 * first.size, bytes_accessed=4 * first.size, transcendentals=0),
        name="combine",
    )(first, second, third)


def on_device(records, w_query, w_key, w_value, pair_owner, pair_partner, confidence, labels):
    recs, seq, width = records.shape
    count = pair_owner.shape[0]
    devices = lax.axis_size(AXES)
    first_id = lax.axis_index(AXES) * recs
    weights = (w_query, w_key, w_value)

    left_records = from_behind(records, 1)
    right_records = from_behind(records, -1)
    own_info = jnp.concatenate(
        [pair_owner - first_id, jnp.mod(pair_partner - first_id, recs * devices), confidence, labels]
    )
    info = from_behind(own_info, 1)
    (own,) = project([records], weights)
    to_left, kept, to_right, loss = pairs(info, own, left_records, right_records, weights, count)
    from_right, from_left = from_behind(to_left, -1), from_behind(to_right, 1)
    loss = column_total(loss)
    met = row_met(loss)
    record_grad, loss = lax.optimization_barrier((combine(from_right, kept, from_left), loss))
    loss = sum(met, loss) / (count * devices)
    return (loss[0, 0], record_grad)


def solution(mesh):
    blocks = P(AXES, None, None)
    in_specs = (blocks, P(), P(), P(), P(AXES), P(AXES), P(AXES), P(AXES))
    return jax.shard_map(
        on_device, mesh=mesh, in_specs=in_specs, out_specs=(P(), blocks), check_vma=False
    )
```
